256 devices in a mesh: wide: 32 (over y, x, core), narrow: 8 (over z).
Axes of the slice: x: 4, y: 4, z: 8, core: 2. Of those that a mesh axis runs over, the one named last changes fastest.
Arguments:
- constraint_rows: bfloat16 [512, 256, 1024], P(None, ('wide', 'narrow')), may hold values from -1 to 1
- metric: bfloat16 [1024, 1024], replicated, may hold values from -8 to 8, as said below
Outputs:
- factored: float32 [512, 256, 8, 128], P(None, 'wide', 'narrow')
The draws below stay inside these ranges and needn't reach their ends.
Inputs may be any that keep to these rules, and one draw needn't show every extreme that they name: `metric`: symmetric and positive definite.
All inputs are finite; a program needn't handle non-finite values.
Results may differ from the reference program's by a relative error of at most 0.0052.
Values may be sent and summed in bfloat16 or wider, within the bound.
No kernel may reach another device: no remote copies, remote signals or barrier semaphores. Data moves between devices by JAX's collectives and lax.ppermute only.
A program may use at most 64 MiB of HBM per device.

```python
import jax
import jax.numpy as jnp
from jax import lax

N = 1024
P_SIZE = 1024
PB = 256
NPANEL = 2
LOCAL = 512
GROUPS = 256
N_NARROW = 8


def draw_constraint_rows(key, part):
    key_common, key_noise, key_scale = jax.random.split(jax.random.fold_in(key, 31), 3)
    common = jax.random.normal(key_common, (N,), jnp.float32)
    noise_draw = jax.random.normal(key_noise, (LOCAL, GROUPS, N), jnp.float32)
    row_scale = jnp.exp(jax.random.uniform(key_scale, (LOCAL, GROUPS, 1), jnp.float32, -0.35, 0.35))
    drawn_rows = row_scale * (0.7 * common + 0.7 * noise_draw) / jnp.sqrt(jnp.float32(N))
    return jnp.clip(drawn_rows, -1.0, 1.0).astype(jnp.bfloat16)


def draw_metric(key, part):
    key_base, key_diag = jax.random.split(jax.random.fold_in(key, 47))
    base_draw = jax.random.normal(key_base, (N, N), jnp.float32)
    gram_part = jnp.dot(base_draw, base_draw.T) / (2.0 * N)
    diag_shift = jax.random.uniform(jax.random.fold_in(key_diag, 5), (N,), jnp.float32, 0.5, 1.5)
    matrix = 0.5 * (gram_part + gram_part.T) + jnp.diag(diag_shift)
    return jnp.clip(matrix, -8.0, 8.0).astype(jnp.bfloat16)


def setup_inputs(seed: int = 0) -> dict:
    splits = jax.random.split(jax.random.key(seed), 3)
    return {
        "constraint_rows": draw_constraint_rows(jax.random.fold_in(splits[2], 71), 0),
        "metric": draw_metric(jax.random.fold_in(splits[2], 71), 0),
    }


def left_solve(factor_low, right_side):
    return jax.scipy.linalg.solve_triangular(factor_low, right_side, lower=True)

def reference(constraint_rows, metric):
    flat_rows = constraint_rows.reshape(LOCAL * GROUPS, N)
    panel_vectors = flat_rows[:P_SIZE]
    projected = jnp.dot(flat_rows.astype(jnp.float32), metric.astype(jnp.float32), preferred_element_type=jnp.float32).astype(jnp.bfloat16)
    gram_cols = jnp.dot(projected.astype(jnp.float32), panel_vectors.T.astype(jnp.float32), preferred_element_type=jnp.float32)
    schur_slab = gram_cols * gram_cols
    for panel_number in range(NPANEL):
        col_begin = panel_number * PB
        col_end = col_begin + PB
        diag_block = schur_slab[col_begin:col_end, col_begin:col_end]
        factor_low = jnp.linalg.cholesky(diag_block)
        upper_part = left_solve(factor_low, schur_slab[col_begin:col_end, col_end:])
        column = left_solve(factor_low, schur_slab[:, col_begin:col_end].T).T
        trailing = schur_slab[:, col_end:] - jnp.dot(column, upper_part, precision=lax.Precision.HIGHEST)
        schur_slab = jnp.concatenate([schur_slab[:, :col_begin], column, trailing], axis=1)
    return schur_slab.reshape(LOCAL, GROUPS, P_SIZE // N_NARROW, N_NARROW).transpose(0, 1, 3, 2)
```

```python
import functools

import jax
import jax.numpy as jnp
from jax import lax
from jax.experimental import pallas as pl
from jax.experimental.pallas import tpu as pltpu
from jax.sharding import PartitionSpec as P

PB = 256
F32 = jnp.float32
BF16 = jnp.bfloat16
HIGHEST = lax.Precision.HIGHEST
VMEM = pl.BlockSpec(memory_space=pltpu.VMEM)


def mm(a, b):
    return jnp.dot(a, b, preferred_element_type=F32)


def mm_nt(a, b):
    return lax.dot_general(a, b, (((1,), (1,)), ((), ())), preferred_element_type=F32)


def fmm(a, b):
    return jnp.dot(a, b, precision=HIGHEST, preferred_element_type=F32)


def fmm_nt(a, b):
    return lax.dot_general(
        a, b, (((1,), (1,)), ((), ())), precision=HIGHEST, preferred_element_type=F32
    )


def square(x):
    return x * x


def over_lanes(x, j):
    return jnp.broadcast_to(x[:, j : j + 1], x.shape)


def over_rows(x, m):
    return jnp.broadcast_to(x[m : m + 1, :], x.shape)


def inverse_factor(matrix, store):
    n = matrix.shape[1]
    tiles = [matrix[8 * i : 8 * i + 8, :] for i in range(n // 8)]
    row = lax.broadcasted_iota(jnp.int32, (8, n), 0)
    lane = lax.broadcasted_iota(jnp.int32, (8, n), 1)
    for b in range(n // 8):
        pivot = tiles[b]
        cols = [over_lanes(pivot, 8 * b + m) for m in range(8)]
        result = jnp.zeros((8, n), F32)
        for m in range(8):
            j = 8 * b + m
            d = over_rows(cols[m], m)
            r = 1.0 / d
            here = row == m
            mult = jnp.where(here, -r, cols[m] * r)
            prow = jnp.where(lane == j, 1.0, over_rows(pivot, m))
            result = jnp.where(here & (lane <= j), prow * lax.rsqrt(d), result)
            pivot = jnp.where(here | (lane == j), 0.0, pivot) - mult * prow
            for k in range(m + 1, 8):
                cols[k] = jnp.where(here, 0.0, cols[k]) - mult * over_rows(cols[k], m)
        store(b, result)
        if b + 1 < n // 8:
            rows = [over_rows(pivot, m) for m in range(8)]
            keep = (lane < 8 * b) | (lane >= 8 * b + 8)
            for i in range(b + 1, n // 8):
                t = [over_lanes(tiles[i], 8 * b + m) * rows[m] for m in range(8)]
                t = ((t[0] + t[1]) + (t[2] + t[3])) + ((t[4] + t[5]) + (t[6] + t[7]))
                tiles[i] = jnp.where(keep, tiles[i], 0.0) - t


def factor_block(block, out_ref, half=128):
    def writer(base):
        def store(i, tile):
            out_ref[base + 8 * i : base + 8 * i + 8, base : base + half] = tile

        return store

    out_ref[:half, half:] = jnp.zeros((half, half), F32)
    inverse_factor(block[:half, :half], writer(0))
    top = out_ref[:half, :half]
    lower = fmm_nt(block[half:, :half], top)
    inverse_factor(block[half:, half:] - fmm_nt(lower, lower), writer(half))
    out_ref[half:, :half] = -fmm(out_ref[half:, half:], fmm(lower, top))


def own_kernel(rows_ref, metric_ref, proj_ref, spread_ref, spread_t_ref):
    proj_ref[...] = mm(rows_ref[...], metric_ref[...]).astype(BF16)
    for ref, cols in ((spread_ref, 256), (spread_t_ref, 512)):
        per = cols // 8
        r = lax.broadcasted_iota(jnp.int32, (1024, 1024), 0)
        c = lax.broadcasted_iota(jnp.int32, (1024, 1024), 1)
        dst, lane = c // 128, c % 128
        want = (lane // per) * cols + (lane % per) * 8 + dst
        ref[...] = jnp.where(r == want, 1.0, 0.0).astype(BF16)


def first_kernel(panel_ref, metric_ref, proj_ref, inv_ref):
    panel = panel_ref[...]
    proj = mm(panel, metric_ref[...]).astype(BF16)
    proj_ref[...] = proj
    diag = square(mm_nt(proj, panel))
    factor_block(0.5 * (diag + diag.T), inv_ref)


def packed(values, groups, spread):
    size = values.shape[0] // groups
    side = jnp.concatenate([values[g * size : (g + 1) * size] for g in range(groups)], axis=1)
    return mm(side.astype(BF16), spread).astype(BF16)


def middle_kernel(
    own_proj_ref, p0_ref, inv_ref, panel_ref, later_ref, metric_ref, spread_ref,
    schur_ref, upper_ref, low_ref, col_ref, send_ref,
):
    v0, v1, inv = panel_ref[...], later_ref[:PB], inv_ref[...]
    col = fmm_nt(square(mm_nt(own_proj_ref[...], v0)), inv)
    col_ref[...] = col
    strips = packed(col, 4, spread_ref[...])
    for s in range(8):
        send_ref[s] = strips[:, 128 * s : 128 * s + 128]
    upper = fmm(inv, square(mm_nt(p0_ref[...], later_ref[...])))
    upper_ref[...] = upper
    p1 = mm(v1, metric_ref[...]).astype(BF16)
    low = fmm_nt(square(mm_nt(p1, v0)), inv)
    low_ref[...] = low
    slab = square(mm_nt(p1, later_ref[...])) - fmm(low, upper)
    schur_ref[...] = slab


def second_kernel(schur_ref, inv_ref):
    diag = schur_ref[:, :PB]
    factor_block(0.5 * (diag + diag.T), inv_ref)


def last_kernel(
    own_proj_ref, later_ref, col_ref, upper_ref, schur_ref, inv_ref, spread_ref, spread_t_ref,
    send_ref,
):
    inv = inv_ref[...]
    slab = square(mm_nt(own_proj_ref[...], later_ref[...])) - fmm(col_ref[...], upper_ref[...])
    col = fmm_nt(slab[:, :PB], inv)
    strips = packed(col, 4, spread_ref[...])
    for s in range(8):
        send_ref[s, :128] = strips[:, 128 * s : 128 * s + 128]
    upper = fmm(inv, schur_ref[:, PB:])
    trail = packed(slab[:, PB:] - fmm(col, upper), 2, spread_t_ref[...])
    for s in range(8):
        send_ref[s, 128:] = trail[:, 128 * s : 128 * s + 128]


def join_kernel(first_ref, rest_ref, out_ref):
    lane = lax.broadcasted_iota(jnp.int32, (128, 128), 1)
    for s in range(8):
        a = first_ref[s].astype(F32)
        b = rest_ref[s, :128].astype(F32)
        t = [rest_ref[s, 128:256].astype(F32), rest_ref[s, 256:].astype(F32)]
        for g in range(4):
            x = pltpu.roll(a, (-32 * g) % 128, 1)
            y = pltpu.roll(b, (32 - 32 * g) % 128, 1)
            z = pltpu.roll(t[g % 2], (64 - 64 * (g // 2)) % 128, 1)
            out_ref[pl.ds(1024 * g + s, 128, stride=8), :] = jnp.where(
                lane < 32, x, jnp.where(lane < 64, y, z)
            )


def call(kernel, outs, flops, name):
    shapes = [jax.ShapeDtypeStruct(s, t) for s, t in outs]
    single = len(shapes) == 1
    return pl.pallas_call(
        kernel,
        out_shape=shapes[0] if single else shapes,
        name=name,
        compiler_params=pltpu.CompilerParams(vmem_limit_bytes=56 << 20),
        cost_estimate=pl.CostEstimate(flops=flops, bytes_accessed=4 << 20, transcendentals=0),
    )


def spread_to(value, count, axis, groups=None):
    wide = jnp.broadcast_to(value[None], (count,) + value.shape)
    return lax.all_to_all(wide, axis, 0, 0, tiled=True, axis_index_groups=groups)


def local(constraint_rows, metric):
    cores = 2
    plane = lax.axis_size("wide") // cores
    narrow = lax.axis_size("narrow")
    same_core = [[cores * i + c for i in range(plane)] for c in range(cores)]
    swap = [(i, i ^ 1) for i in range(plane * cores)]
    core = lax.axis_index("wide") % cores
    rows = constraint_rows[:, 0, :]
    row_count, n = rows.shape

    def gathered(block):
        mine = spread_to(block, plane, "wide", same_core)
        other = lax.ppermute(mine, "wide", swap)
        return jnp.where(
            core == 0, jnp.stack([mine, other], 1), jnp.stack([other, mine], 1)
        )

    column = spread_to(rows[:4], narrow, "narrow")
    own_proj, spread, spread_t = call(
        own_kernel, [((row_count, n), BF16), ((1024, 1024), BF16), ((1024, 1024), BF16)], 4 << 30, "own"
    )(rows, metric)
    panel = gathered(column[:, 0]).reshape(PB, n)
    later = gathered(column[:, 1:].transpose(1, 0, 2))
    later = later.transpose(2, 0, 1, 3, 4).reshape(3 * PB, n)
    p0, inv0 = call(first_kernel, [((PB, n), BF16), ((PB, PB), F32)], 16 << 30, "first")(panel, metric)
    schur, upper, low, col, send0 = call(
        middle_kernel,
        [((PB, 3 * PB), F32), ((PB, 3 * PB), F32), ((PB, PB), F32), ((row_count, PB), F32), ((8, 128, 128), BF16)],
        4 << 30, "middle",
    )(own_proj, p0, inv0, panel, later, metric, spread)
    got0 = lax.all_to_all(send0, "narrow", 0, 0, tiled=True)
    inv1 = call(second_kernel, [((PB, PB), F32)], 16 << 30, "second")(schur)
    send1 = call(last_kernel, [((8, 384, 128), BF16)], 4 << 30, "last")(
        own_proj, later, col, upper, schur, inv1, spread, spread_t
    )
    got1 = lax.all_to_all(send1, "narrow", 0, 0, tiled=True)
    out = call(join_kernel, [((row_count * 8, 128), F32)], 1 << 30, "join")(got0, got1)
    return out.reshape(row_count, 8, 1, 128)


def solution(mesh):
    placed = (P(None, ("wide", "narrow"), None), P())
    return jax.shard_map(
        local,
        mesh=mesh,
        in_specs=placed,
        out_specs=P(None, "wide", "narrow", None),
        check_vma=False,
    )
```

```python
import functools

import jax
import jax.numpy as jnp
from jax import lax
from jax.experimental import pallas as pl
from jax.experimental.pallas import tpu as pltpu
from jax.sharding import PartitionSpec as P

PB = 256
F32 = jnp.float32
BF16 = jnp.bfloat16


def mm(a, b):
    return jnp.dot(a, b, preferred_element_type=F32)


def mm_nt(a, b):
    return lax.dot_general(a, b, (((1,), (1,)), ((), ())), preferred_element_type=F32)


def square(x):
    return x * x


def split(x):
    high = x.astype(BF16)
    return high, (x - high.astype(F32)).astype(BF16)


def fmm(a, b):
    (ah, al), (bh, bl) = split(a), split(b)
    return mm(ah, bh) + (mm(ah, bl) + mm(al, bh))


def fmm_nt(a, b):
    (ah, al), (bh, bl) = split(a), split(b)
    return mm_nt(ah, bh) + (mm_nt(ah, bl) + mm_nt(al, bh))


def over_lanes(x, j):
    return jnp.broadcast_to(x[:, j : j + 1], x.shape)


def over_rows(x, m):
    return jnp.broadcast_to(x[m : m + 1, :], x.shape)


def inverse_factor(matrix, store, between):
    n = matrix.shape[1]
    tiles = [matrix[8 * i : 8 * i + 8, :] for i in range(n // 8)]
    row = lax.broadcasted_iota(jnp.int32, (8, n), 0)
    lane = lax.broadcasted_iota(jnp.int32, (8, n), 1)
    one = tiles[0] * 0.0 + 1.0
    for b in range(n // 8):
        pivot = tiles[b]
        cols = [over_lanes(pivot, 8 * b + m) * one for m in range(8)]
        result = jnp.zeros((8, n), F32)
        for m in range(8):
            j = 8 * b + m
            d = over_rows(cols[m], m)
            r = 1.0 / d
            here = row == m
            mult = jnp.where(here, -r, cols[m] * r)
            prow = jnp.where(lane == j, 1.0, over_rows(pivot, m))
            result = jnp.where(here & (lane <= j), prow * lax.rsqrt(d), result)
            pivot = jnp.where(here | (lane == j), 0.0, pivot) - mult * prow
            for k in range(m + 1, 8):
                cols[k] = jnp.where(here, 0.0, cols[k]) - mult * over_rows(cols[k], m)
        store(b, result)
        between()
        if b + 1 < n // 8:
            rows = [over_rows(pivot, m) for m in range(8)]
            keep = (lane // 8) != b
            for i in range(b + 1, n // 8):
                t = [over_lanes(tiles[i], 8 * b + m) * rows[m] for m in range(8)]
                t = ((t[0] + t[1]) + (t[2] + t[3])) + ((t[4] + t[5]) + (t[6] + t[7]))
                tiles[i] = jnp.where(keep, tiles[i], 0.0) - t


def factor_block(block, out_ref, jobs, half=128):
    jobs = list(jobs)
    steps = 2 * half // 8
    count = [0, 0]

    def between():
        count[0] += 1
        while count[1] < len(jobs) and count[1] * (steps - 2) < count[0] * len(jobs):
            jobs[count[1]]()
            count[1] += 1

    def writer(base):
        def store(i, tile):
            out_ref[base + 8 * i : base + 8 * i + 8, base : base + half] = tile

        return store

    out_ref[:half, half:] = jnp.zeros((half, half), F32)
    inverse_factor(block[:half, :half], writer(0), between)
    top = out_ref[:half, :half]
    lower = fmm_nt(block[half:, :half], top)
    inverse_factor(block[half:, half:] - fmm_nt(lower, lower), writer(half), between)
    out_ref[half:, :half] = -fmm(out_ref[half:, half:], fmm(lower, top))


def own_kernel(rows_ref, metric_ref, proj_ref, spread_ref, spread_t_ref):
    proj_ref[...] = mm(rows_ref[...], metric_ref[...]).astype(BF16)
    for ref, cols in ((spread_ref, 256), (spread_t_ref, 512)):
        per = cols // 8
        r = lax.broadcasted_iota(jnp.int32, (1024, 1024), 0)
        c = lax.broadcasted_iota(jnp.int32, (1024, 1024), 1)
        dst, lane = c // 128, c % 128
        want = (lane // per) * cols + (lane % per) * 8 + dst
        ref[...] = jnp.where(r == want, 1.0, 0.0).astype(BF16)


def first_kernel(panel_ref, metric_ref, own_proj_ref, inv_ref, head_ref, own_ref, proj_ref):
    proj_ref[:PB] = mm(panel_ref[:PB], metric_ref[...]).astype(BF16)
    diag = square(mm_nt(proj_ref[:PB], panel_ref[:PB]))

    def project():
        proj_ref[PB:] = mm(panel_ref[PB : 2 * PB], metric_ref[...]).astype(BF16)

    def slab(out, rows, r, c):
        def job():
            out[r : r + PB, c : c + PB] = square(
                mm_nt(rows[r : r + PB], panel_ref[c : c + PB])
            )

        return job

    jobs = [project]
    jobs += [slab(own_ref, own_proj_ref, r, c) for c in range(0, 1024, PB) for r in (0, PB)]
    jobs += [slab(head_ref, proj_ref, r, c) for r in (0, PB) for c in range(0, 1024, PB) if r + c]
    factor_block(0.5 * (diag + diag.T), inv_ref, jobs)


def packed(values, groups, spread):
    size = values.shape[0] // groups
    side = jnp.concatenate([values[g * size : (g + 1) * size] for g in range(groups)], axis=1)
    return mm(side.astype(BF16), spread).astype(BF16)


def second_kernel(inv0_ref, head_ref, own_ref, inv_ref, own1_ref, upper1_ref, col_ref, upper_ref):
    inv0 = inv0_ref[...]
    upper_ref[:, :PB] = fmm(inv0, head_ref[:PB, PB : 2 * PB])
    low = fmm_nt(head_ref[PB:, :PB], inv0)
    diag = head_ref[PB:, PB : 2 * PB] - fmm(low, upper_ref[:, :PB])

    def column(r):
        def job():
            col_ref[r : r + PB] = fmm_nt(own_ref[r : r + PB, :PB], inv0)

        return job

    def top(c):
        def job():
            upper_ref[:, c : c + PB] = fmm(inv0, head_ref[:PB, PB + c : 2 * PB + c])

        return job

    def under(c):
        def job():
            upper1_ref[:, c - PB : c] = head_ref[PB:, PB + c : 2 * PB + c] - fmm(
                low, upper_ref[:, c : c + PB]
            )

        return job

    def rest(r, c):
        def job():
            own1_ref[r : r + PB, c : c + PB] = own_ref[r : r + PB, PB + c : 2 * PB + c] - fmm(
                col_ref[r : r + PB], upper_ref[:, c : c + PB]
            )

        return job

    jobs = [column(0), column(PB), top(PB), top(2 * PB), under(PB), under(2 * PB)]
    jobs += [rest(r, c) for c in range(0, 768, PB) for r in (0, PB)]
    factor_block(0.5 * (diag + diag.T), inv_ref, jobs)


def last_kernel(own1_ref, upper1_ref, col_ref, inv_ref, spread_ref, spread_t_ref, send_ref):
    inv = inv_ref[...]
    col = fmm_nt(own1_ref[:, :PB], inv)
    upper = fmm(inv, upper1_ref[...])
    trail = packed(own1_ref[:, PB:] - fmm(col, upper), 2, spread_t_ref[...])
    first = packed(col_ref[...], 4, spread_ref[...])
    strips = packed(col, 4, spread_ref[...])
    for s in range(8):
        send_ref[s, :128] = first[:, 128 * s : 128 * s + 128]
        send_ref[s, 128:256] = strips[:, 128 * s : 128 * s + 128]
        send_ref[s, 256:] = trail[:, 128 * s : 128 * s + 128]


def join_kernel(got_ref, out_ref):
    group = pl.program_id(0)
    lane = lax.broadcasted_iota(jnp.int32, (128, 128), 1)
    for s in range(8):
        a, b = got_ref[s, :128].astype(F32), got_ref[s, 128:256].astype(F32)
        t = got_ref[s, pl.ds(256 + 128 * (group % 2), 128)].astype(F32)
        x = pltpu.roll(a, (128 - 32 * group) % 128, 1)
        y = pltpu.roll(b, (160 - 32 * group) % 128, 1)
        z = pltpu.roll(t, (192 - 64 * (group // 2)) % 128, 1)
        out_ref[pl.ds(s, 128, stride=8), :] = jnp.where(
            lane < 32, x, jnp.where(lane < 64, y, z)
        )


def call(kernel, outs, flops, name, scratch=(), **more):
    shapes = [jax.ShapeDtypeStruct(s, t) for s, t in outs]
    return pl.pallas_call(
        kernel,
        out_shape=shapes[0] if len(shapes) == 1 else shapes,
        scratch_shapes=[pltpu.VMEM(s, t) for s, t in scratch],
        name=name,
        compiler_params=pltpu.CompilerParams(vmem_limit_bytes=56 << 20),
        cost_estimate=pl.CostEstimate(flops=flops, bytes_accessed=4 << 20, transcendentals=0),
        **more,
    )


def spread_to(value, count, axis, groups=None):
    wide = jnp.broadcast_to(value[None], (count,) + value.shape)
    return lax.all_to_all(wide, axis, 0, 0, tiled=True, axis_index_groups=groups)


def local(constraint_rows, metric):
    cores = 2
    plane = lax.axis_size("wide") // cores
    narrow = lax.axis_size("narrow")
    same_core = [[cores * i + c for i in range(plane)] for c in range(cores)]
    swap = [(i, i ^ 1) for i in range(plane * cores)]
    core = lax.axis_index("wide") % cores
    rows = constraint_rows[:, 0, :]
    row_count, n = rows.shape

    def gathered(block):
        mine = spread_to(block, plane, "wide", same_core)
        other = lax.ppermute(mine, "wide", swap)
        return jnp.where(
            core == 0, jnp.stack([mine, other], 1), jnp.stack([other, mine], 1)
        )

    column = spread_to(rows[:4], narrow, "narrow").transpose(1, 0, 2)
    own_proj, spread, spread_t = call(
        own_kernel, [((row_count, n), BF16), ((1024, 1024), BF16), ((1024, 1024), BF16)], 8 << 30, "own"
    )(rows, metric)
    mine = spread_to(column, plane, "wide", same_core)
    mine, own_proj = lax.optimization_barrier((mine, own_proj))
    other = lax.ppermute(mine, "wide", swap)
    panel = jnp.where(core == 0, jnp.stack([mine, other], 1), jnp.stack([other, mine], 1))
    panel = panel.transpose(2, 0, 1, 3, 4).reshape(4 * PB, n)
    inv0, head, own = call(
        first_kernel,
        [((PB, PB), F32), ((2 * PB, 4 * PB), F32), ((row_count, 4 * PB), F32)],
        16 << 30, "first", [((2 * PB, n), BF16)],
    )(panel, metric, own_proj)
    inv1, own1, upper1, col = call(
        second_kernel,
        [((PB, PB), F32), ((row_count, 3 * PB), F32), ((PB, 2 * PB), F32), ((row_count, PB), F32)],
        16 << 30, "second", [((PB, 3 * PB), F32)],
    )(inv0, head, own)
    send = call(last_kernel, [((8, 512, 128), BF16)], 4 << 30, "last")(
        own1, upper1, col, inv1, spread, spread_t
    )
    got = lax.all_to_all(send, "narrow", 0, 0, tiled=True)
    out = call(
        join_kernel, [((row_count * 8, 128), F32)], 1 << 30, "join",
        grid=(4,), in_specs=[pl.BlockSpec((8, 512, 128), lambda g: (0, 0, 0))],
        out_specs=pl.BlockSpec((1024, 128), lambda g: (g, 0)),
    )(got)
    return out.reshape(row_count, 8, 1, 128)


def solution(mesh):
    placed = (P(None, ("wide", "narrow"), None), P())
    return jax.shard_map(
        local,
        mesh=mesh,
        in_specs=placed,
        out_specs=P(None, "wide", "narrow", None),
        check_vma=False,
    )
```

```python
import functools

import jax
import jax.numpy as jnp
from jax import lax
from jax.experimental import pallas as pl
from jax.experimental.pallas import tpu as pltpu
from jax.sharding import PartitionSpec as P

PB = 256
F32 = jnp.float32
BF16 = jnp.bfloat16


def mm(a, b):
    return jnp.dot(a, b, preferred_element_type=F32)


def mm_nt(a, b):
    return lax.dot_general(a, b, (((1,), (1,)), ((), ())), preferred_element_type=F32)


def square(x):
    return x * x


def split(x):
    high = x.astype(BF16)
    return high, (x - high.astype(F32)).astype(BF16)


def fmm(a, b):
    (ah, al), (bh, bl) = split(a), split(b)
    return mm(ah, bh) + (mm(ah, bl) + mm(al, bh))


def fmm_nt(a, b):
    (ah, al), (bh, bl) = split(a), split(b)
    return mm_nt(ah, bh) + (mm_nt(ah, bl) + mm_nt(al, bh))


def over_lanes(x, j):
    return jnp.broadcast_to(x[:, j : j + 1], x.shape)


def over_rows(x, m):
    return jnp.broadcast_to(x[m : m + 1, :], x.shape)


def inverse_factor(matrix, store, between):
    n = matrix.shape[1]
    tiles = [matrix[8 * i : 8 * i + 8, :] for i in range(n // 8)]
    row = lax.broadcasted_iota(jnp.int32, (8, n), 0)
    lane = lax.broadcasted_iota(jnp.int32, (8, n), 1)
    one = tiles[0] * 0.0 + 1.0
    for b in range(n // 8):
        pivot = tiles[b]
        cols = [over_lanes(pivot, 8 * b + m) * one for m in range(8)]
        result = jnp.zeros((8, n), F32)
        for m in range(8):
            j = 8 * b + m
            d = over_rows(cols[m], m)
            r = 1.0 / d
            here = row == m
            mult = jnp.where(here, -r, cols[m] * r)
            prow = jnp.where(lane == j, 1.0, over_rows(pivot, m))
            result = jnp.where(here & (lane <= j), prow * lax.rsqrt(d), result)
            pivot = jnp.where(here | (lane == j), 0.0, pivot) - mult * prow
            for k in range(m + 1, 8):
                cols[k] = jnp.where(here, 0.0, cols[k]) - mult * over_rows(cols[k], m)
        store(b, result)
        between()
        if b + 1 < n // 8:
            rows = [over_rows(pivot, m) for m in range(8)]
            keep = (lane // 8) != b
            for i in range(b + 1, n // 8):
                t = [over_lanes(tiles[i], 8 * b + m) * rows[m] for m in range(8)]
                t = ((t[0] + t[1]) + (t[2] + t[3])) + ((t[4] + t[5]) + (t[6] + t[7]))
                tiles[i] = jnp.where(keep, tiles[i], 0.0) - t


def factor_block(block, out_ref, jobs, half=128):
    jobs = list(jobs)
    steps = 2 * half // 8
    count = [0, 0]

    def between():
        count[0] += 1
        while count[1] < len(jobs) and count[1] * (steps - 2) < count[0] * len(jobs):
            jobs[count[1]]()
            count[1] += 1

    def writer(base):
        def store(i, tile):
            out_ref[base + 8 * i : base + 8 * i + 8, base : base + half] = tile

        return store

    out_ref[:half, half:] = jnp.zeros((half, half), F32)
    inverse_factor(block[:half, :half], writer(0), between)
    top = out_ref[:half, :half]
    lower = fmm_nt(block[half:, :half], top)
    inverse_factor(block[half:, half:] - fmm_nt(lower, lower), writer(half), between)
    out_ref[half:, :half] = -fmm(out_ref[half:, half:], fmm(lower, top))


def own_kernel(rows_ref, metric_ref, proj_ref, spread_ref, spread_t_ref):
    proj_ref[...] = mm(rows_ref[...], metric_ref[...]).astype(BF16)
    for ref, cols in ((spread_ref, 256), (spread_t_ref, 512)):
        per = cols // 8
        r = lax.broadcasted_iota(jnp.int32, (1024, 1024), 0)
        c = lax.broadcasted_iota(jnp.int32, (1024, 1024), 1)
        dst, lane = c // 128, c % 128
        want = (lane // per) * cols + (lane % per) * 8 + dst
        ref[...] = jnp.where(r == want, 1.0, 0.0).astype(BF16)


def packed(values, groups, spread):
    size = values.shape[0] // groups
    side = jnp.concatenate([values[g * size : (g + 1) * size] for g in range(groups)], axis=1)
    return mm(side.astype(BF16), spread).astype(BF16)


def core_kernel(
    core_ref, mine_ref, other_ref, metric_hbm, own_proj_hbm, spread_hbm, spread_t_hbm, send_ref,
    panel_ref, metric_ref, own_proj_ref, spread_ref, spread_t_ref, proj_ref, head_ref, own_ref,
    own1_ref, upper_ref, upper1_ref, col_ref, inv0_ref, inv1_ref, sems,
):
    pairs = (
        (metric_hbm, metric_ref), (own_proj_hbm, own_proj_ref),
        (spread_hbm, spread_ref), (spread_t_hbm, spread_t_ref),
    )
    copies = [pltpu.make_async_copy(x, y, sems.at[i]) for i, (x, y) in enumerate(pairs)]
    for copy in copies:
        copy.start()
    first_core = core_ref[0] == 0
    for k in range(4):
        for i in range(16):
            x, y = mine_ref[i, k].astype(F32), other_ref[i, k].astype(F32)
            low, high = jnp.where(first_core, x, y), jnp.where(first_core, y, x)
            panel_ref[256 * k + 16 * i : 256 * k + 16 * i + 16] = jnp.concatenate(
                [low, high], axis=0
            ).astype(BF16)
    copies[0].wait()
    proj_ref[:PB] = mm(panel_ref[:PB], metric_ref[...]).astype(BF16)
    diag = square(mm_nt(proj_ref[:PB], panel_ref[:PB]))
    copies[1].wait()

    def project():
        proj_ref[PB:] = mm(panel_ref[PB : 2 * PB], metric_ref[...]).astype(BF16)

    def slab(out, rows, r, c):
        def job():
            out[r : r + PB, c : c + PB] = square(
                mm_nt(rows[r : r + PB], panel_ref[c : c + PB])
            )

        return job

    jobs = [project]
    jobs += [slab(own_ref, own_proj_ref, r, c) for c in range(0, 1024, PB) for r in (0, PB)]
    jobs += [slab(head_ref, proj_ref, r, c) for r in (0, PB) for c in range(0, 1024, PB) if r + c]
    factor_block(0.5 * (diag + diag.T), inv0_ref, jobs)
    copies[2].wait()
    copies[3].wait()

    inv0 = inv0_ref[...]
    upper_ref[:, :PB] = fmm(inv0, head_ref[:PB, PB : 2 * PB])
    low = fmm_nt(head_ref[PB:, :PB], inv0)
    diag = head_ref[PB:, PB : 2 * PB] - fmm(low, upper_ref[:, :PB])

    def column(r):
        def job():
            col_ref[r : r + PB] = fmm_nt(own_ref[r : r + PB, :PB], inv0)

        return job

    def top(c):
        def job():
            upper_ref[:, c : c + PB] = fmm(inv0, head_ref[:PB, PB + c : 2 * PB + c])

        return job

    def under(c):
        def job():
            upper1_ref[:, c - PB : c] = head_ref[PB:, PB + c : 2 * PB + c] - fmm(
                low, upper_ref[:, c : c + PB]
            )

        return job

    def rest(r, c):
        def job():
            own1_ref[r : r + PB, c : c + PB] = own_ref[r : r + PB, PB + c : 2 * PB + c] - fmm(
                col_ref[r : r + PB], upper_ref[:, c : c + PB]
            )

        return job

    def finished():
        strips = packed(col_ref[...], 4, spread_ref[...])
        for s in range(8):
            send_ref[s, :128] = strips[:, 128 * s : 128 * s + 128]

    jobs = [column(0), column(PB), top(PB), top(2 * PB), under(PB), under(2 * PB)]
    jobs += [rest(r, c) for c in range(0, 768, PB) for r in (0, PB)] + [finished]
    factor_block(0.5 * (diag + diag.T), inv1_ref, jobs)

    inv = inv1_ref[...]
    col = fmm_nt(own1_ref[:, :PB], inv)
    upper = fmm(inv, upper1_ref[...])
    trail = packed(own1_ref[:, PB:] - fmm(col, upper), 2, spread_t_ref[...])
    strips = packed(col, 4, spread_ref[...])
    for s in range(8):
        send_ref[s, 128:256] = strips[:, 128 * s : 128 * s + 128]
        send_ref[s, 256:] = trail[:, 128 * s : 128 * s + 128]


def join_kernel(got_ref, out_ref):
    group = pl.program_id(0)
    lane = lax.broadcasted_iota(jnp.int32, (128, 128), 1)
    parts = []
    for s in range(8):
        a, b = got_ref[s, :128].astype(F32), got_ref[s, 128:256].astype(F32)
        t = got_ref[s, pl.ds(256 + 128 * (group % 2), 128)].astype(F32)
        x = pltpu.roll(a, (128 - 32 * group) % 128, 1)
        y = pltpu.roll(b, (160 - 32 * group) % 128, 1)
        z = pltpu.roll(t, (192 - 64 * (group // 2)) % 128, 1)
        parts.append(jnp.where(lane < 32, x, jnp.where(lane < 64, y, z)))
    stacked = jnp.stack(parts, 0)
    out_ref[...] = pltpu.einshape("skl->ksl", stacked).reshape(1024, 128)


def call(kernel, outs, flops, name, scratch=(), sems=(), **more):
    shapes = [jax.ShapeDtypeStruct(s, t) for s, t in outs]
    return pl.pallas_call(
        kernel,
        out_shape=shapes[0] if len(shapes) == 1 else shapes,
        scratch_shapes=[pltpu.VMEM(s, t) for s, t in scratch] + list(sems),
        name=name,
        compiler_params=pltpu.CompilerParams(vmem_limit_bytes=48 << 20),
        cost_estimate=pl.CostEstimate(flops=flops, bytes_accessed=4 << 20, transcendentals=0),
        **more,
    )


def spread_to(value, count, axis, groups=None):
    wide = jnp.broadcast_to(value[None], (count,) + value.shape)
    return lax.all_to_all(wide, axis, 0, 0, tiled=True, axis_index_groups=groups)


def local(constraint_rows, metric):
    cores = 2
    plane = lax.axis_size("wide") // cores
    narrow = lax.axis_size("narrow")
    same_core = [[cores * i + c for i in range(plane)] for c in range(cores)]
    swap = [(i, i ^ 1) for i in range(plane * cores)]
    core = lax.axis_index("wide") % cores
    rows = constraint_rows[:, 0, :]
    row_count, n = rows.shape

    def gathered(block):
        mine = spread_to(block, plane, "wide", same_core)
        other = lax.ppermute(mine, "wide", swap)
        return jnp.where(
            core == 0, jnp.stack([mine, other], 1), jnp.stack([other, mine], 1)
        )

    column = spread_to(rows[:4], narrow, "narrow").transpose(1, 0, 2)
    own_proj, spread, spread_t = call(
        own_kernel, [((row_count, n), BF16), ((1024, 1024), BF16), ((1024, 1024), BF16)], 8 << 30, "own"
    )(rows, metric)
    mine = spread_to(column, plane, "wide", same_core)
    mine, own_proj = lax.optimization_barrier((mine, own_proj))
    other = lax.ppermute(mine, "wide", swap)
    hbm, vmem = pl.BlockSpec(memory_space=pl.ANY), pl.BlockSpec(memory_space=pltpu.VMEM)
    send = call(
        core_kernel, [((8, row_count, 128), BF16)], 16 << 30, "core",
        [
            ((4 * PB, n), BF16), ((n, n), BF16), ((row_count, n), BF16), ((1024, 1024), BF16),
            ((1024, 1024), BF16), ((2 * PB, n), BF16), ((2 * PB, 4 * PB), F32),
            ((row_count, 4 * PB), F32), ((row_count, 3 * PB), F32), ((PB, 3 * PB), F32),
            ((PB, 2 * PB), F32), ((row_count, PB), F32), ((PB, PB), F32), ((PB, PB), F32),
        ],
        [pltpu.SemaphoreType.DMA((4,))],
        in_specs=[pl.BlockSpec(memory_space=pltpu.SMEM), vmem, vmem, hbm, hbm, hbm, hbm],
    )(core.reshape(1), mine, other, metric, own_proj, spread, spread_t)
    got = lax.all_to_all(send, "narrow", 0, 0, tiled=True)
    out = call(
        join_kernel, [((row_count * 8, 128), F32)], 1 << 30, "join",
        grid=(4,), in_specs=[pl.BlockSpec((8, 512, 128), lambda g: (0, 0, 0))],
        out_specs=pl.BlockSpec((1024, 128), lambda g: (g, 0)),
    )(got)
    return out.reshape(row_count, 8, 1, 128)


def solution(mesh):
    placed = (P(None, ("wide", "narrow"), None), P())
    return jax.shard_map(
        local,
        mesh=mesh,
        in_specs=placed,
        out_specs=P(None, "wide", "narrow", None),
        check_vma=False,
    )
```

```python
import functools

import jax
import jax.numpy as jnp
from jax import lax
from jax.experimental import pallas as pl
from jax.experimental.pallas import tpu as pltpu
from jax.sharding import PartitionSpec as P

PB = 256
F32 = jnp.float32
BF16 = jnp.bfloat16


def mm(a, b):
    return jnp.dot(a, b, preferred_element_type=F32)


def mm_nt(a, b):
    return lax.dot_general(a, b, (((1,), (1,)), ((), ())), preferred_element_type=F32)


def square(x):
    return x * x


def split(x):
    high = x.astype(BF16)
    return high, (x - high.astype(F32)).astype(BF16)


def fmm(a, b):
    (ah, al), (bh, bl) = split(a), split(b)
    return mm(ah, bh) + (mm(ah, bl) + mm(al, bh))


def fmm_nt(a, b):
    (ah, al), (bh, bl) = split(a), split(b)
    return mm_nt(ah, bh) + (mm_nt(ah, bl) + mm_nt(al, bh))


def over_lanes(x, j):
    return jnp.broadcast_to(x[:, j : j + 1], x.shape)


def over_rows(x, m):
    return jnp.broadcast_to(x[m : m + 1, :], x.shape)


def tree_sum(terms):
    while len(terms) > 1:
        terms = [x + y for x, y in zip(terms[::2], terms[1::2], strict=True)]
    return terms[0]


def inverse_factor(matrix, store, between):
    n = matrix.shape[1]
    steps = n // 8
    tiles = [matrix[8 * i : 8 * i + 8, :] for i in range(steps)]
    row = lax.broadcasted_iota(jnp.int32, (8, n), 0)
    lane = lax.broadcasted_iota(jnp.int32, (8, n), 1)
    one = tiles[0] * 0.0 + 1.0

    def columns(tile, b):
        return [over_lanes(tile, 8 * b + m) * one for m in range(8)]

    cols = columns(tiles[0], 0)
    for b in range(steps):
        pivot, more = tiles[b], b + 1 < steps
        if more:
            ahead = columns(pivot, b + 1)
            below, below_ahead = columns(tiles[b + 1], b), columns(tiles[b + 1], b + 1)
        result = jnp.zeros((8, n), F32)
        for m in range(8):
            j = 8 * b + m
            d = over_rows(cols[m], m)
            r = 1.0 / d
            here = row == m
            mult = jnp.where(here, -r, cols[m] * r)
            prow = jnp.where(lane == j, 1.0, over_rows(pivot, m))
            result = jnp.where(here & (lane <= j), prow * lax.rsqrt(d), result)
            pivot = jnp.where(here | (lane == j), 0.0, pivot) - mult * prow
            for k in range(m + 1, 8):
                cols[k] = jnp.where(here, 0.0, cols[k]) - mult * over_rows(cols[k], m)
            if more:
                for k in range(8):
                    ahead[k] = jnp.where(here, 0.0, ahead[k]) - mult * over_rows(ahead[k], m)
        store(b, result)
        between()
        if more:
            cols = [
                below_ahead[k] - tree_sum([below[m] * over_rows(ahead[k], m) for m in range(8)])
                for k in range(8)
            ]
            rows = [over_rows(pivot, m) for m in range(8)]
            keep = (lane // 8) != b
            for i in range(b + 1, steps):
                at = below if i == b + 1 else [over_lanes(tiles[i], 8 * b + m) for m in range(8)]
                tiles[i] = jnp.where(keep, tiles[i], 0.0) - tree_sum(
                    [at[m] * rows[m] for m in range(8)]
                )


def factor_block(block, out_ref, jobs, half=128):
    jobs = list(jobs)
    steps = 2 * half // 8
    count = [0, 0]

    def between():
        count[0] += 1
        while count[1] < len(jobs) and count[1] * (steps - 2) < count[0] * len(jobs):
            jobs[count[1]]()
            count[1] += 1

    def writer(base):
        def store(i, tile):
            out_ref[base + 8 * i : base + 8 * i + 8, base : base + half] = tile

        return store

    out_ref[:half, half:] = jnp.zeros((half, half), F32)
    inverse_factor(block[:half, :half], writer(0), between)
    top = out_ref[:half, :half]
    lower = fmm_nt(block[half:, :half], top)
    inverse_factor(block[half:, half:] - fmm_nt(lower, lower), writer(half), between)
    out_ref[half:, :half] = -fmm(out_ref[half:, half:], fmm(lower, top))


def own_kernel(rows_ref, metric_ref, proj_ref, spread_ref, spread_t_ref):
    proj_ref[...] = mm(rows_ref[...], metric_ref[...]).astype(BF16)
    for ref, cols in ((spread_ref, 256), (spread_t_ref, 512)):
        per = cols // 8
        r = lax.broadcasted_iota(jnp.int32, (1024, 1024), 0)
        c = lax.broadcasted_iota(jnp.int32, (1024, 1024), 1)
        dst, lane = c // 128, c % 128
        want = (lane // per) * cols + (lane % per) * 8 + dst
        ref[...] = jnp.where(r == want, 1.0, 0.0).astype(BF16)


def packed(values, groups, spread):
    size = values.shape[0] // groups
    side = jnp.concatenate([values[g * size : (g + 1) * size] for g in range(groups)], axis=1)
    return mm(side.astype(BF16), spread).astype(BF16)


def core_kernel(
    core_ref, mine_ref, other_ref, metric_hbm, own_proj_hbm, spread_hbm, spread_t_hbm, send_ref,
    panel_ref, metric_ref, own_proj_ref, spread_ref, spread_t_ref, proj_ref, head_ref, own_ref,
    own1_ref, upper_ref, upper1_ref, col_ref, inv0_ref, inv1_ref, sems,
):
    pairs = (
        (metric_hbm, metric_ref), (own_proj_hbm, own_proj_ref),
        (spread_hbm, spread_ref), (spread_t_hbm, spread_t_ref),
    )
    copies = [pltpu.make_async_copy(x, y, sems.at[i]) for i, (x, y) in enumerate(pairs)]
    for copy in copies:
        copy.start()
    first_core = core_ref[0] == 0
    for k in range(4):
        for i in range(16):
            x, y = mine_ref[i, k].astype(F32), other_ref[i, k].astype(F32)
            low, high = jnp.where(first_core, x, y), jnp.where(first_core, y, x)
            panel_ref[256 * k + 16 * i : 256 * k + 16 * i + 16] = jnp.concatenate(
                [low, high], axis=0
            ).astype(BF16)
    copies[0].wait()
    proj_ref[:PB] = mm(panel_ref[:PB], metric_ref[...]).astype(BF16)
    diag = square(mm_nt(proj_ref[:PB], panel_ref[:PB]))
    copies[1].wait()

    def project():
        proj_ref[PB:] = mm(panel_ref[PB : 2 * PB], metric_ref[...]).astype(BF16)

    def slab(out, rows, r, c):
        def job():
            out[r : r + PB, c : c + PB] = square(
                mm_nt(rows[r : r + PB], panel_ref[c : c + PB])
            )

        return job

    jobs = [project]
    jobs += [slab(own_ref, own_proj_ref, r, c) for c in range(0, 1024, PB) for r in (0, PB)]
    jobs += [slab(head_ref, proj_ref, r, c) for r in (0, PB) for c in range(0, 1024, PB) if r + c]
    factor_block(0.5 * (diag + diag.T), inv0_ref, jobs)
    copies[2].wait()
    copies[3].wait()

    inv0 = inv0_ref[...]
    upper_ref[:, :PB] = fmm(inv0, head_ref[:PB, PB : 2 * PB])
    low = fmm_nt(head_ref[PB:, :PB], inv0)
    diag = head_ref[PB:, PB : 2 * PB] - fmm(low, upper_ref[:, :PB])

    def column(r):
        def job():
            col_ref[r : r + PB] = fmm_nt(own_ref[r : r + PB, :PB], inv0)

        return job

    def top(c):
        def job():
            upper_ref[:, c : c + PB] = fmm(inv0, head_ref[:PB, PB + c : 2 * PB + c])

        return job

    def under(c):
        def job():
            upper1_ref[:, c - PB : c] = head_ref[PB:, PB + c : 2 * PB + c] - fmm(
                low, upper_ref[:, c : c + PB]
            )

        return job

    def rest(r, c):
        def job():
            own1_ref[r : r + PB, c : c + PB] = own_ref[r : r + PB, PB + c : 2 * PB + c] - fmm(
                col_ref[r : r + PB], upper_ref[:, c : c + PB]
            )

        return job

    def finished():
        strips = packed(col_ref[...], 4, spread_ref[...])
        for s in range(8):
            send_ref[s, :128] = strips[:, 128 * s : 128 * s + 128]

    jobs = [column(0), column(PB), top(PB), top(2 * PB), under(PB), under(2 * PB)]
    jobs += [rest(r, c) for c in range(0, 768, PB) for r in (0, PB)] + [finished]
    factor_block(0.5 * (diag + diag.T), inv1_ref, jobs)

    inv = inv1_ref[...]
    col = fmm_nt(own1_ref[:, :PB], inv)
    upper = fmm(inv, upper1_ref[...])
    trail = packed(own1_ref[:, PB:] - fmm(col, upper), 2, spread_t_ref[...])
    strips = packed(col, 4, spread_ref[...])
    for s in range(8):
        send_ref[s, 128:256] = strips[:, 128 * s : 128 * s + 128]
        send_ref[s, 256:] = trail[:, 128 * s : 128 * s + 128]


def join_kernel(got_ref, out_ref):
    group = pl.program_id(0)
    lane = lax.broadcasted_iota(jnp.int32, (128, 128), 1)
    parts = []
    for s in range(8):
        a, b = got_ref[s, :128].astype(F32), got_ref[s, 128:256].astype(F32)
        t = got_ref[s, pl.ds(256 + 128 * (group % 2), 128)].astype(F32)
        x = pltpu.roll(a, (128 - 32 * group) % 128, 1)
        y = pltpu.roll(b, (160 - 32 * group) % 128, 1)
        z = pltpu.roll(t, (192 - 64 * (group // 2)) % 128, 1)
        parts.append(jnp.where(lane < 32, x, jnp.where(lane < 64, y, z)))
    stacked = jnp.stack(parts, 0)
    out_ref[...] = pltpu.einshape("skl->ksl", stacked).reshape(1024, 128)


def call(kernel, outs, flops, name, scratch=(), sems=(), **more):
    shapes = [jax.ShapeDtypeStruct(s, t) for s, t in outs]
    return pl.pallas_call(
        kernel,
        out_shape=shapes[0] if len(shapes) == 1 else shapes,
        scratch_shapes=[pltpu.VMEM(s, t) for s, t in scratch] + list(sems),
        name=name,
        compiler_params=pltpu.CompilerParams(vmem_limit_bytes=48 << 20),
        cost_estimate=pl.CostEstimate(flops=flops, bytes_accessed=4 << 20, transcendentals=0),
        **more,
    )


def spread_to(value, count, axis, groups=None):
    wide = jnp.broadcast_to(value[None], (count,) + value.shape)
    return lax.all_to_all(wide, axis, 0, 0, tiled=True, axis_index_groups=groups)


def local(constraint_rows, metric):
    cores = 2
    plane = lax.axis_size("wide") // cores
    narrow = lax.axis_size("narrow")
    same_core = [[cores * i + c for i in range(plane)] for c in range(cores)]
    swap = [(i, i ^ 1) for i in range(plane * cores)]
    core = lax.axis_index("wide") % cores
    rows = constraint_rows[:, 0, :]
    row_count, n = rows.shape

    def gathered(block):
        mine = spread_to(block, plane, "wide", same_core)
        other = lax.ppermute(mine, "wide", swap)
        return jnp.where(
            core == 0, jnp.stack([mine, other], 1), jnp.stack([other, mine], 1)
        )

    column = spread_to(rows[:4], narrow, "narrow").transpose(1, 0, 2)
    own_proj, spread, spread_t = call(
        own_kernel, [((row_count, n), BF16), ((1024, 1024), BF16), ((1024, 1024), BF16)], 8 << 30, "own"
    )(rows, metric)
    mine = spread_to(column, plane, "wide", same_core)
    mine, own_proj = lax.optimization_barrier((mine, own_proj))
    other = lax.ppermute(mine, "wide", swap)
    hbm, vmem = pl.BlockSpec(memory_space=pl.ANY), pl.BlockSpec(memory_space=pltpu.VMEM)
    send = call(
        core_kernel, [((8, row_count, 128), BF16)], 16 << 30, "core",
        [
            ((4 * PB, n), BF16), ((n, n), BF16), ((row_count, n), BF16), ((1024, 1024), BF16),
            ((1024, 1024), BF16), ((2 * PB, n), BF16), ((2 * PB, 4 * PB), F32),
            ((row_count, 4 * PB), F32), ((row_count, 3 * PB), F32), ((PB, 3 * PB), F32),
            ((PB, 2 * PB), F32), ((row_count, PB), F32), ((PB, PB), F32), ((PB, PB), F32),
        ],
        [pltpu.SemaphoreType.DMA((4,))],
        in_specs=[pl.BlockSpec(memory_space=pltpu.SMEM), vmem, vmem, hbm, hbm, hbm, hbm],
    )(core.reshape(1), mine, other, metric, own_proj, spread, spread_t)
    got = lax.all_to_all(send, "narrow", 0, 0, tiled=True)
    out = call(
        join_kernel, [((row_count * 8, 128), F32)], 1 << 30, "join",
        grid=(4,), in_specs=[pl.BlockSpec((8, 512, 128), lambda g: (0, 0, 0))],
        out_specs=pl.BlockSpec((1024, 128), lambda g: (g, 0)),
    )(got)
    return out.reshape(row_count, 8, 1, 128)


def solution(mesh):
    placed = (P(None, ("wide", "narrow"), None), P())
    return jax.shard_map(
        local,
        mesh=mesh,
        in_specs=placed,
        out_specs=P(None, "wide", "narrow", None),
        check_vma=False,
    )
```

```python
import functools

import jax
import jax.numpy as jnp
from jax import lax
from jax.experimental import pallas as pl
from jax.experimental.pallas import tpu as pltpu
from jax.sharding import PartitionSpec as P

PB = 256
F32 = jnp.float32
BF16 = jnp.bfloat16


def mm(a, b):
    return jnp.dot(a, b, preferred_element_type=F32)


def mm_nt(a, b):
    return lax.dot_general(a, b, (((1,), (1,)), ((), ())), preferred_element_type=F32)


def square(x):
    return x * x


def split(x):
    high = x.astype(BF16)
    return high, (x - high.astype(F32)).astype(BF16)


def fmm(a, b):
    (ah, al), (bh, bl) = split(a), split(b)
    return mm(ah, bh) + (mm(ah, bl) + mm(al, bh))


def fmm_nt(a, b):
    (ah, al), (bh, bl) = split(a), split(b)
    return mm_nt(ah, bh) + (mm_nt(ah, bl) + mm_nt(al, bh))


def over_lanes(x, j):
    return jnp.broadcast_to(x[:, j : j + 1], x.shape)


def over_rows(x, m):
    return jnp.broadcast_to(x[m : m + 1, :], x.shape)


def tree_sum(terms):
    while len(terms) > 1:
        terms = [x + y for x, y in zip(terms[::2], terms[1::2], strict=True)]
    return terms[0]


def inverse_factor(matrix, store, between):
    n = matrix.shape[1]
    steps = n // 8
    tiles = [matrix[8 * i : 8 * i + 8, :] for i in range(steps)]
    row = lax.broadcasted_iota(jnp.int32, (8, n), 0)
    lane = lax.broadcasted_iota(jnp.int32, (8, n), 1)
    one = tiles[0] * 0.0 + 1.0

    def columns(tile, b):
        return [over_lanes(tile, 8 * b + m) * one for m in range(8)]

    cols = columns(tiles[0], 0)
    for b in range(steps):
        pivot, more = tiles[b], b + 1 < steps
        if more:
            ahead = columns(pivot, b + 1)
            below, below_ahead = columns(tiles[b + 1], b), columns(tiles[b + 1], b + 1)
        result = jnp.zeros((8, n), F32)
        for m in range(8):
            j = 8 * b + m
            d = over_rows(cols[m], m)
            r = 1.0 / d
            here = row == m
            mult = jnp.where(here, -r, cols[m] * r)
            prow = jnp.where(lane == j, 1.0, over_rows(pivot, m))
            result = jnp.where(here & (lane <= j), prow * lax.rsqrt(d), result)
            pivot = jnp.where(here | (lane == j), 0.0, pivot) - mult * prow
            for k in range(m + 1, 8):
                cols[k] = jnp.where(here, 0.0, cols[k]) - mult * over_rows(cols[k], m)
            if more:
                for k in range(8):
                    ahead[k] = jnp.where(here, 0.0, ahead[k]) - mult * over_rows(ahead[k], m)
        store(b, result)
        between()
        if more:
            cols = [
                below_ahead[k] - tree_sum([below[m] * over_rows(ahead[k], m) for m in range(8)])
                for k in range(8)
            ]
            rows = [over_rows(pivot, m) for m in range(8)]
            keep = (lane // 8) != b
            for i in range(b + 1, steps):
                at = below if i == b + 1 else [over_lanes(tiles[i], 8 * b + m) for m in range(8)]
                tiles[i] = jnp.where(keep, tiles[i], 0.0) - tree_sum(
                    [at[m] * rows[m] for m in range(8)]
                )


def factor_block(block, out_ref, jobs, half=128):
    jobs = list(jobs)
    steps = 2 * half // 8
    count = [0, 0]

    def between():
        count[0] += 1
        while count[1] < len(jobs) and count[1] * (steps - 2) < count[0] * len(jobs):
            jobs[count[1]]()
            count[1] += 1

    def writer(base):
        def store(i, tile):
            out_ref[base + 8 * i : base + 8 * i + 8, base : base + half] = tile

        return store

    out_ref[:half, half:] = jnp.zeros((half, half), F32)
    inverse_factor(block[:half, :half], writer(0), between)
    top = out_ref[:half, :half]
    lower = fmm_nt(block[half:, :half], top)
    inverse_factor(block[half:, half:] - fmm_nt(lower, lower), writer(half), between)
    out_ref[half:, :half] = -fmm(out_ref[half:, half:], fmm(lower, top))


def own_kernel(rows_ref, metric_ref, proj_ref, spread_ref):
    proj_ref[...] = mm(rows_ref[...], metric_ref[...]).astype(BF16)
    r = lax.broadcasted_iota(jnp.int32, (1024, 1024), 0)
    c = lax.broadcasted_iota(jnp.int32, (1024, 1024), 1)
    spread_ref[...] = jnp.where(r == (c % 128) * 8 + c // 128, 1.0, 0.0).astype(BF16)


def core_kernel(
    core_ref, mine_ref, other_ref, metric_hbm, own_proj_hbm, spread_hbm, send_ref,
    panel_ref, metric_ref, own_proj_ref, spread_ref, proj_ref, head_ref, own_ref,
    own1_ref, upper_ref, upper1_ref, col_ref, inv0_ref, inv1_ref, sems,
):
    pairs = (
        (metric_hbm, metric_ref), (own_proj_hbm, own_proj_ref),
        (spread_hbm, spread_ref),
    )
    copies = [pltpu.make_async_copy(x, y, sems.at[i]) for i, (x, y) in enumerate(pairs)]
    for copy in copies:
        copy.start()
    first_core = core_ref[0] == 0
    for k in range(4):
        for i in range(16):
            x, y = mine_ref[i, k].astype(F32), other_ref[i, k].astype(F32)
            low, high = jnp.where(first_core, x, y), jnp.where(first_core, y, x)
            panel_ref[256 * k + 16 * i : 256 * k + 16 * i + 16] = jnp.concatenate(
                [low, high], axis=0
            ).astype(BF16)
    copies[0].wait()
    proj_ref[:PB] = mm(panel_ref[:PB], metric_ref[...]).astype(BF16)
    diag = square(mm_nt(proj_ref[:PB], panel_ref[:PB]))
    copies[1].wait()

    def project():
        proj_ref[PB:] = mm(panel_ref[PB : 2 * PB], metric_ref[...]).astype(BF16)

    def slab(out, rows, r, c):
        def job():
            out[r : r + PB, c : c + PB] = square(
                mm_nt(rows[r : r + PB], panel_ref[c : c + PB])
            )

        return job

    jobs = [project]
    jobs += [slab(own_ref, own_proj_ref, r, c) for c in range(0, 1024, PB) for r in (0, PB)]
    jobs += [slab(head_ref, proj_ref, r, c) for r in (0, PB) for c in range(0, 1024, PB) if r + c]
    factor_block(0.5 * (diag + diag.T), inv0_ref, jobs)
    copies[2].wait()

    inv0 = inv0_ref[...]
    upper_ref[:, :PB] = fmm(inv0, head_ref[:PB, PB : 2 * PB])
    low = fmm_nt(head_ref[PB:, :PB], inv0)
    diag = head_ref[PB:, PB : 2 * PB] - fmm(low, upper_ref[:, :PB])

    def column(r):
        def job():
            col_ref[r : r + PB] = fmm_nt(own_ref[r : r + PB, :PB], inv0)

        return job

    def top(c):
        def job():
            upper_ref[:, c : c + PB] = fmm(inv0, head_ref[:PB, PB + c : 2 * PB + c])

        return job

    def under(c):
        def job():
            upper1_ref[:, c - PB : c] = head_ref[PB:, PB + c : 2 * PB + c] - fmm(
                low, upper_ref[:, c : c + PB]
            )

        return job

    def rest(r, c):
        def job():
            own1_ref[r : r + PB, c : c + PB] = own_ref[r : r + PB, PB + c : 2 * PB + c] - fmm(
                col_ref[r : r + PB], upper_ref[:, c : c + PB]
            )

        return job

    def finished():
        strips = mm(col_ref[...].astype(BF16), spread_ref[:PB]).astype(BF16)
        for s in range(8):
            send_ref[s] = strips[:, 128 * s : 128 * s + 128]

    jobs = [column(0), column(PB), top(PB), top(2 * PB), under(PB), under(2 * PB)]
    jobs += [rest(r, c) for c in range(0, 768, PB) for r in (0, PB)] + [finished]
    factor_block(0.5 * (diag + diag.T), inv1_ref, jobs)

    inv = inv1_ref[...]
    col = fmm_nt(own1_ref[:, :PB], inv)
    upper = fmm(inv, upper1_ref[...])
    trail = own1_ref[:, PB:] - fmm(col, upper)
    strips = mm(jnp.concatenate([col.astype(BF16), trail.astype(BF16)], axis=1), spread_ref[PB:])
    for s in range(8):
        send_ref[s] = (strips[:, 128 * s : 128 * s + 128] + send_ref[s].astype(F32)).astype(BF16)


def join_kernel(got_ref, out_ref):
    stacked = got_ref[...].astype(F32)
    out_ref[...] = pltpu.einshape("skl->ksl", stacked).reshape(out_ref.shape)


def call(kernel, outs, flops, name, scratch=(), sems=(), **more):
    shapes = [jax.ShapeDtypeStruct(s, t) for s, t in outs]
    return pl.pallas_call(
        kernel,
        out_shape=shapes[0] if len(shapes) == 1 else shapes,
        scratch_shapes=[pltpu.VMEM(s, t) for s, t in scratch] + list(sems),
        name=name,
        compiler_params=pltpu.CompilerParams(vmem_limit_bytes=48 << 20),
        cost_estimate=pl.CostEstimate(flops=flops, bytes_accessed=4 << 20, transcendentals=0),
        **more,
    )


def spread_to(value, count, axis, groups=None):
    wide = jnp.broadcast_to(value[None], (count,) + value.shape)
    return lax.all_to_all(wide, axis, 0, 0, tiled=True, axis_index_groups=groups)


def local(constraint_rows, metric):
    cores = 2
    plane = lax.axis_size("wide") // cores
    narrow = lax.axis_size("narrow")
    same_core = [[cores * i + c for i in range(plane)] for c in range(cores)]
    swap = [(i, i ^ 1) for i in range(plane * cores)]
    core = lax.axis_index("wide") % cores
    rows = constraint_rows[:, 0, :]
    row_count, n = rows.shape

    def gathered(block):
        mine = spread_to(block, plane, "wide", same_core)
        other = lax.ppermute(mine, "wide", swap)
        return jnp.where(
            core == 0, jnp.stack([mine, other], 1), jnp.stack([other, mine], 1)
        )

    column = spread_to(rows[:4], narrow, "narrow").transpose(1, 0, 2)
    own_proj, spread = call(
        own_kernel, [((row_count, n), BF16), ((1024, 1024), BF16)], 8 << 30, "own"
    )(rows, metric)
    mine = spread_to(column, plane, "wide", same_core)
    mine, own_proj = lax.optimization_barrier((mine, own_proj))
    other = lax.ppermute(mine, "wide", swap)
    hbm, vmem = pl.BlockSpec(memory_space=pl.ANY), pl.BlockSpec(memory_space=pltpu.VMEM)
    send = call(
        core_kernel, [((8, row_count, 128), BF16)], 16 << 30, "core",
        [
            ((4 * PB, n), BF16), ((n, n), BF16), ((row_count, n), BF16), ((1024, 1024), BF16),
            ((2 * PB, n), BF16), ((2 * PB, 4 * PB), F32),
            ((row_count, 4 * PB), F32), ((row_count, 3 * PB), F32), ((PB, 3 * PB), F32),
            ((PB, 2 * PB), F32), ((row_count, PB), F32), ((PB, PB), F32), ((PB, PB), F32),
        ],
        [pltpu.SemaphoreType.DMA((3,))],
        in_specs=[pl.BlockSpec(memory_space=pltpu.SMEM), vmem, vmem, hbm, hbm, hbm],
    )(core.reshape(1), mine, other, metric, own_proj, spread)
    got = lax.all_to_all(send, "narrow", 0, 0, tiled=True)
    out = call(
        join_kernel, [((row_count * 8, 128), F32)], 1 << 30, "join",
        grid=(4,), in_specs=[pl.BlockSpec((8, 128, 128), lambda g: (0, g, 0))],
        out_specs=pl.BlockSpec((1024, 128), lambda g: (g, 0)),
    )(got)
    return out.reshape(row_count, 8, 1, 128)


def solution(mesh):
    placed = (P(None, ("wide", "narrow"), None), P())
    return jax.shard_map(
        local,
        mesh=mesh,
        in_specs=placed,
        out_specs=P(None, "wide", "narrow", None),
        check_vma=False,
    )
```
